512 devices in a mesh: occ: 128 (over y, z, core), virt: 4 (over x).
Axes of the slice: x: 4, y: 8, z: 8, core: 2. Of those that a mesh axis runs over, the one named last changes fastest.
Arguments:
- factors: bfloat16 [768, 98304], P('virt', 'occ'), may hold values from -1 to 1
- occ_energy: float32 [64], replicated, may hold values from -2 to -0.5
- virt_energy: float32 [768], replicated, may hold values from 0.2 to 3
- pair_table: int32 [256, 2], P('occ'), may hold values from 0 to 63, as said below
- pair_count: int32 [128], P('occ'), may hold values from 0 to 2, as said below
Outputs:
- gamma: float32 [768, 98304], P('virt', 'occ')
The draws below stay inside these ranges and needn't reach their ends.
Inputs may be any that keep to these rules, and one draw needn't show every extreme that they name: `pair_table`: each row holds two different orbitals. `pair_count`: the counts sum to exactly 128, and some host has exactly 2.
All inputs are finite; a program needn't handle non-finite values.
Results may differ from the reference program's by a relative error of at most 0.0029.
Values may be sent and summed in bfloat16 or wider, within the bound.
A program may use at most 64 MiB of HBM per device.

```python
import jax
import jax.numpy as jnp
from jax import lax

O = 64
V = 768
NAUX = 1536
LOAD = 2
PAIRS = 128
N_OCC = 128


def draw_pair_table(key, part):
    key = jax.random.fold_in(key, 11)
    first_key, shift_key = jax.random.split(key)
    first = jax.random.randint(first_key, (N_OCC * LOAD,), 0, O)
    offset = jax.random.randint(shift_key, (N_OCC * LOAD,), 1, O)
    second = (first + offset) % O
    return jnp.stack([first, second], axis=1).astype(jnp.int32)


def draw_pair_count(key, part):
    key = jax.random.fold_in(key, 23)
    full_key, order_key = jax.random.split(key)
    busiest = jax.random.randint(full_key, (), 0, N_OCC)
    scores = jax.random.permutation(order_key, N_OCC * LOAD).astype(jnp.int32)
    slots = jnp.arange(N_OCC * LOAD, dtype=jnp.int32)
    owners = slots // LOAD
    scores = jnp.where(owners == busiest, slots % LOAD - LOAD, scores)
    ranking = jnp.argsort(jnp.argsort(scores, stable=True), stable=True)
    taken = (ranking < PAIRS).astype(jnp.int32)
    return jnp.sum(taken.reshape(N_OCC, LOAD), axis=1).astype(jnp.int32)


def steps_of(own_key, extent, cuts, smallest, top_value):
    factor_of, own = 1.0, jax.random.fold_in(own_key, 6)
    for dim, parts in cuts:
        heights = jnp.exp(jax.random.uniform(jax.random.fold_in(own, dim), (parts,), jnp.float32, smallest / len(cuts), top_value / len(cuts)))
        factor_of = factor_of * jnp.repeat(heights, extent[dim] // parts).reshape([-1 if axis == dim else 1 for axis in range(len(extent))])
    return factor_of


def normal_values(stream_key, extent, width, reach, cuts=(), kind=jnp.bfloat16):
    values = jax.random.normal(stream_key, extent, jnp.float32) * width
    if len(cuts) > 0:
        values = steps_of(stream_key, extent, cuts, -0.22, 0.18) * values
    return jnp.clip(values, min=-reach, max=reach).astype(kind)


def setup_inputs(seed: int = 0) -> dict:
    key_list = jax.random.split(jax.random.key(seed), 6)
    factors = normal_values(key_list[0], (V, NAUX * O), 0.16, 1.0, ((0, 4), (1, 128)))
    occ_energy = jnp.clip(jax.random.uniform(key_list[1], (O,), jnp.float32, -2.0, -0.5), -2.0, -0.5)
    virt_energy = jnp.clip(jax.random.uniform(key_list[2], (V,), jnp.float32, 0.2, 3.0), 0.2, 3.0)
    pair_table = draw_pair_table(jax.random.fold_in(key_list[5], 71), 0)
    pair_count = draw_pair_count(jax.random.fold_in(key_list[5], 71), 0)
    return dict(factors=factors, occ_energy=occ_energy, virt_energy=virt_energy, pair_table=pair_table, pair_count=pair_count)


def pair_terms(factors, occ_energy, virt_energy, first, second):
    left = lax.dynamic_index_in_dim(factors, first, 0, keepdims=False)
    right = lax.dynamic_index_in_dim(factors, second, 0, keepdims=False)
    couple = lax.dot_general(left, right, (((0,), (0,)), ((), ())), preferred_element_type=jnp.float32)
    energy_sum = jnp.take(occ_energy, first) + jnp.take(occ_energy, second)
    ampl = couple / (energy_sum - virt_energy[:, None] - virt_energy[None, :])
    mixed = (2.0 * ampl - ampl.T).astype(jnp.bfloat16)
    toward_first = lax.dot_general(right, mixed, (((1,), (1,)), ((), ())), preferred_element_type=jnp.float32)
    toward_second = jnp.dot(left, mixed, preferred_element_type=jnp.float32)
    return toward_first.astype(jnp.bfloat16), toward_second.astype(jnp.bfloat16)


def reference(factors, occ_energy, virt_energy, pair_table, pair_count):
    cube = factors.reshape(V, NAUX, O).transpose(2, 1, 0)
    entries = jnp.arange(N_OCC * LOAD, dtype=jnp.int32)
    active = (entries % LOAD) < jnp.repeat(pair_count, LOAD)
    ranking = jnp.cumsum(active.astype(jnp.int32)) - 1
    targets = jnp.arange(PAIRS, dtype=jnp.int32)
    select = (active[None, :] & (ranking[None, :] == targets[:, None])).astype(jnp.int32)
    chosen = jnp.sum(select[:, :, None] * pair_table[None, :, :], axis=1).astype(jnp.int32)

    def step(accumulated, row):
        first = row[0]
        second = row[1]
        toward_first, toward_second = pair_terms(cube, occ_energy, virt_energy, first, second)
        accumulated = accumulated.at[first].add(toward_first.astype(jnp.float32))
        accumulated = accumulated.at[second].add(toward_second.astype(jnp.float32))
        return accumulated, None

    start = jnp.zeros(cube.shape, jnp.float32)
    result, _ = lax.scan(step, start, chosen)
    return result.transpose(2, 1, 0).reshape(V, NAUX * O)
```

```python
import functools

import jax
import jax.numpy as jnp
from jax import lax
from jax.experimental import pallas as pl
from jax.experimental.pallas import tpu as pltpu
from jax.sharding import PartitionSpec as P

BF = jnp.bfloat16
F32 = jnp.float32
SIDE = 8
HOSTS = 32
CHUNK = 16


def nt(a, b):
    return lax.dot_general(a, b, (((1,), (1,)), ((), ())), preferred_element_type=F32)


def tn(a, b):
    return lax.dot_general(a, b, (((0,), (0,)), ((), ())), preferred_element_type=F32)


def nn(a, b):
    return jnp.dot(a, b, preferred_element_type=F32)


def swing(t):
    return (2 * (t % 2) - 1) * ((t + 1) // 2)


def column(rows, shape):
    return lax.broadcasted_iota(jnp.int32, shape, rows)


def whole(ref, sem):
    return pltpu.make_async_copy(ref, ref, sem)


def kernel(dims, tab, cnt, occ_ref, virt_ref, f_ref, out_ref, held, table, onehot, picked,
           got, pairs, spread, diff, mixed, back, summed, grams, hop_out, hop_in, last_out, last_in,
           sem_own, xs, xr, ts, tr, fs, fr, bs, br, gs, gr):
    devices, aux, orbitals, slab, virtuals = dims
    me = lax.axis_index("occ")
    plane = lax.axis_index("virt")
    right, left, opposite = (plane + 1) % 4, (plane + 3) % 4, (plane + 2) % 4
    my_y = me // (2 * SIDE)
    my_z = (me // 2) % SIDE
    my_host = my_y * (SIDE // 2) + my_z // 2
    is_host = ((me % 2) + (my_z + my_y) % 2) == 0
    message = 2 * aux
    tiles = message // 8
    rows = HOSTS * message

    barrier = pltpu.get_barrier_semaphore()

    def greet(t, c):
        pl.semaphore_signal(barrier, inc=1, device_id={"occ": (me + t) % devices})
        return c

    pl.semaphore_signal(barrier, inc=1, device_id={"virt": right})
    pl.semaphore_signal(barrier, inc=1, device_id={"virt": left})
    lax.fori_loop(1, devices, greet, 0)
    pl.semaphore_wait(barrier, devices + 1)

    own = pltpu.make_async_copy(f_ref, held.at[plane], sem_own)
    own.start()
    to_right = pltpu.make_async_remote_copy(f_ref, held.at[plane], xs.at[0], xr.at[0], device_id={"virt": right})
    to_left = pltpu.make_async_remote_copy(f_ref, held.at[plane], xs.at[1], xr.at[1], device_id={"virt": left})
    to_right.start()
    to_left.start()

    lane = lax.broadcasted_iota(jnp.int32, (1, 128), 1)
    line = jnp.where(lane == 4, cnt[0], 0)
    for at, (l, s) in enumerate(((0, 0), (0, 1), (1, 0), (1, 1))):
        line = jnp.where(lane == at, tab[l, s] + 1, line)
    table[me] = line

    def tell(t, c):
        pltpu.make_async_remote_copy(
            table.at[me], table.at[me], ts, tr, device_id={"occ": (me + t) % devices}
        ).start()
        return c

    lax.fori_loop(1, devices, tell, 0)
    half = held.shape[1] // 2
    to_right.wait_recv()
    pass_right = pltpu.make_async_remote_copy(
        held.at[left, pl.ds(0, half)], held.at[left, pl.ds(0, half)], xs.at[2], xr.at[2], device_id={"virt": right})
    pass_right.start()
    to_left.wait_recv()
    pass_left = pltpu.make_async_remote_copy(
        held.at[right, pl.ds(half, half)], held.at[right, pl.ds(half, half)], xs.at[3], xr.at[3], device_id={"virt": left})
    pass_left.start()

    whole(table.at[pl.ds(0, devices - 1)], tr).wait()
    listed = table[...].reshape(devices, 128).astype(F32)
    listed_b = listed.astype(BF)
    flipped = listed.T
    count_row = flipped[4:5, :]
    before = (column(0, (128, 128)) < column(1, (128, 128))).astype(F32).astype(BF)
    rank_row = nn(jnp.broadcast_to(count_row, (16, 128)).astype(BF), before)[0:1, :]

    row = column(0, (rows, 1))
    of_host = (row * 2731) // 65536
    inside = row - of_host * message
    second = inside >= aux
    aux_of = jnp.where(second, inside - aux, inside)
    wanted = (of_host + plane * HOSTS).astype(F32)
    pick0 = ((rank_row == wanted) & (count_row > 0.5)).astype(F32).astype(BF)
    pick1 = ((rank_row + 1.0 == wanted) & (count_row > 1.5)).astype(F32).astype(BF)
    found0 = nn(pick0, listed_b)
    found1 = nn(pick1, listed_b)
    orbital = jnp.where(second, found0[:, 1:2] + found1[:, 3:4], found0[:, 0:1] + found1[:, 2:3])
    key = jnp.where(orbital > 0.5, (aux_of * orbitals).astype(F32) + orbital - 1.0, -1.0)
    onehot[...] = (column(1, (rows, aux * orbitals)).astype(F32) == key).astype(F32).astype(BF)

    own.wait()
    pass_right.wait_recv()
    pass_left.wait_recv()
    picked[...] = nt(onehot[...], held[...].reshape(virtuals, aux * orbitals)).reshape(picked.shape).astype(BF)

    def send(t, c):
        y = (my_y + swing(t // 4) + SIDE) % SIDE
        k = y * 4 + (t + my_z) % 4
        dest = (y * SIDE + 2 * (k % 4) + y % 2) * 2
        src = picked.at[pl.ds(k * tiles, tiles)]
        dst = got.at[pl.ds(me * tiles, tiles)]

        @pl.when(dest != me)
        def _():
            pltpu.make_async_remote_copy(src, dst, fs, fr.at[my_y], device_id={"occ": dest}).start()

        @pl.when(dest == me)
        def _():
            pltpu.make_async_copy(src, dst, fr.at[my_y]).start()

        return c

    lax.fori_loop(0, HOSTS, send, 0)

    part = CHUNK * aux
    block = CHUNK * tiles

    @pl.when(is_host)
    def _():
        mine_at = (my_host + plane * HOSTS).astype(F32)
        hit0 = jnp.where((rank_row == mine_at) & (count_row > 0.5), 1.0, 0.0)
        hit1 = jnp.where((rank_row + 1.0 == mine_at) & (count_row > 1.5), 1.0, 0.0)
        first_at = jnp.sum(hit0 * flipped[0:1, :] + hit1 * flipped[2:3, :], axis=1, keepdims=True)
        second_at = jnp.sum(hit0 * flipped[1:2, :] + hit1 * flipped[3:4, :], axis=1, keepdims=True)
        names = (lax.broadcasted_iota(jnp.int32, (1, orbitals), 1) + 1).astype(F32)
        energy = jnp.sum(
            jnp.where(names == first_at, occ_ref[...], 0.0), axis=1, keepdims=True
        ) + jnp.sum(jnp.where(names == second_at, occ_ref[...], 0.0), axis=1, keepdims=True)
        virt_row = virt_ref[...]
        virt_col = jnp.broadcast_to(virt_row, (128, virtuals)).T[:, 0:1]
        spread[...] = 1.0 / (energy - virt_col - virt_row)
        diff[...] = jnp.zeros_like(diff)

        r = column(0, (2 * part, 2 * part))
        c = column(1, (2 * part, 2 * part))
        low = r >= part
        q = jnp.where(low, r - part, r)
        n = (q * 5462) // 65536
        place = n * message + (q - n * aux) + jnp.where(low, 0, aux)
        sorter = (place == c).astype(F32).astype(BF)

        def collect(t, carry):
            g = (my_y - swing(t) + SIDE) % SIDE
            spot = got.at[pl.ds(g * block, block)]
            whole(spot, fr.at[g]).wait()
            here = nn(sorter, spot[...].reshape(2 * part, virtuals)).astype(BF)
            pairs[g] = here
            over = jnp.concatenate([here[part:] * 2.0, -here[:part]], axis=0).astype(BF)
            diff[...] += tn(over, here)
            return carry

        lax.fori_loop(0, SIDE, collect, 0)
        mixed[...] = (diff[...] * spread[...]).astype(BF)

        def give(t, carry):
            g = (my_y + swing(t) + SIDE) % SIDE
            block_b = pairs[g]
            toward_first = nt(block_b[:part], mixed[...]).astype(BF)
            toward_second = nn(block_b[part:], mixed[...]).astype(BF)
            both = jnp.concatenate([toward_second, toward_first], axis=0)
            back[pl.ds(g * block, block)] = tn(sorter, both).reshape(block, 8, virtuals).astype(BF)

            def out(u, cc):
                dest = g * CHUNK + (u + me) % CHUNK
                src = back.at[pl.ds(dest * tiles, tiles)]
                dst = summed.at[pl.ds(my_host * tiles, tiles)]

                @pl.when(dest != me)
                def _():
                    pltpu.make_async_remote_copy(src, dst, bs, br, device_id={"occ": dest}).start()

                @pl.when(dest == me)
                def _():
                    pltpu.make_async_copy(src, dst, br).start()

                return cc

            lax.fori_loop(0, CHUNK, out, 0)
            return carry

        lax.fori_loop(0, SIDE, give, 0)

    whole(summed, br).wait()
    grams[...] = tn(summed[...].reshape(rows, virtuals), onehot[...]).reshape(grams.shape)

    cut = slab // 2
    hop_out[...] = grams[opposite].astype(BF)
    hop_right = pltpu.make_async_remote_copy(
        hop_out.at[pl.ds(0, cut)], hop_in.at[pl.ds(0, cut)], gs.at[0], gr.at[0], device_id={"virt": right})
    hop_left = pltpu.make_async_remote_copy(
        hop_out.at[pl.ds(cut, cut)], hop_in.at[pl.ds(cut, cut)], gs.at[1], gr.at[1], device_id={"virt": left})
    hop_right.start()
    hop_left.start()
    hop_right.wait_recv()
    last_out[0, pl.ds(0, cut)] = (grams[right, pl.ds(0, cut)] + hop_in[pl.ds(0, cut)].astype(F32)).astype(BF)
    last_out[0, pl.ds(cut, cut)] = grams[right, pl.ds(cut, cut)].astype(BF)
    end_right = pltpu.make_async_remote_copy(
        last_out.at[0], last_in.at[0], gs.at[2], gr.at[2], device_id={"virt": right})
    end_right.start()
    hop_left.wait_recv()
    last_out[1, pl.ds(0, cut)] = grams[left, pl.ds(0, cut)].astype(BF)
    last_out[1, pl.ds(cut, cut)] = (grams[left, pl.ds(cut, cut)] + hop_in[pl.ds(cut, cut)].astype(F32)).astype(BF)
    end_left = pltpu.make_async_remote_copy(
        last_out.at[1], last_in.at[1], gs.at[3], gr.at[3], device_id={"virt": left})
    end_left.start()

    to_right.wait_send()
    to_left.wait_send()
    pass_right.wait_send()
    pass_left.wait_send()
    whole(table.at[pl.ds(0, devices - 1)], ts).wait()

    @pl.when(is_host)
    def _():
        whole(picked.at[pl.ds(0, (HOSTS - 1) * tiles)], fs).wait()
        whole(back.at[pl.ds(0, (devices - 1) * tiles)], bs).wait()

    @pl.when(jnp.logical_not(is_host))
    def _():
        whole(picked, fs).wait()

    end_right.wait_recv()
    end_left.wait_recv()
    out_ref[...] = grams[plane] + last_in[0].astype(F32) + last_in[1].astype(F32)
    hop_right.wait_send()
    hop_left.wait_send()
    end_right.wait_send()
    end_left.wait_send()


def body(factors, occ_energy, virt_energy, pair_table, pair_count):
    devices = lax.axis_size("occ")
    orbitals = occ_energy.shape[0]
    virtuals = virt_energy.shape[0]
    slab, width = factors.shape
    aux = width // orbitals
    message = 2 * aux
    tiles = message // 8
    rows = HOSTS * message
    part = CHUNK * aux
    dims = (devices, aux, orbitals, slab, virtuals)
    dma = pltpu.SemaphoreType.DMA
    vmem = pl.BlockSpec(memory_space=pltpu.VMEM)
    smem = pl.BlockSpec(memory_space=pltpu.SMEM)
    return pl.pallas_call(
        functools.partial(kernel, dims),
        out_shape=jax.ShapeDtypeStruct((slab, width), F32),
        in_specs=[smem, smem, vmem, vmem, pl.BlockSpec(memory_space=pl.ANY)],
        out_specs=vmem,
        scratch_shapes=[
            pltpu.VMEM((4, slab // 8, 8, width), BF),
            pltpu.VMEM((devices, 1, 128), jnp.int32),
            pltpu.VMEM((rows, width), BF),
            pltpu.VMEM((HOSTS * tiles, 8, virtuals), BF),
            pltpu.VMEM((devices * tiles, 8, virtuals), BF),
            pltpu.VMEM((SIDE, 2 * part, virtuals), BF),
            pltpu.VMEM((virtuals, virtuals), F32),
            pltpu.VMEM((virtuals, virtuals), F32),
            pltpu.VMEM((virtuals, virtuals), BF),
            pltpu.VMEM((devices * tiles, 8, virtuals), BF),
            pltpu.VMEM((HOSTS * tiles, 8, virtuals), BF),
            pltpu.VMEM((4, slab, width), F32),
            pltpu.VMEM((slab, width), BF),
            pltpu.VMEM((slab, width), BF),
            pltpu.VMEM((2, slab, width), BF),
            pltpu.VMEM((2, slab, width), BF),
            dma(()), dma((4,)), dma((4,)), dma(()), dma(()), dma(()), dma((SIDE,)), dma(()), dma(()),
            dma((4,)), dma((4,)),
        ],
        compiler_params=pltpu.CompilerParams(
            collective_id=0, has_side_effects=True, vmem_limit_bytes=60 * 1024 * 1024
        ),
    )(pair_table, pair_count, occ_energy.reshape(1, -1), virt_energy.reshape(1, -1),
      factors.reshape(slab // 8, 8, width))


def solution(mesh):
    in_specs = (P("virt", "occ"), P(), P(), P("occ", None), P("occ"))
    out_specs = P("virt", "occ")
    return jax.shard_map(body, mesh=mesh, in_specs=in_specs, out_specs=out_specs, check_vma=False)
```

```python
import functools

import jax
import jax.numpy as jnp
from jax import lax
from jax.experimental import pallas as pl
from jax.experimental.pallas import tpu as pltpu
from jax.sharding import PartitionSpec as P

BF = jnp.bfloat16
F32 = jnp.float32
SIDE = 8
HOSTS = SIDE * SIDE
CHUNK = 2 * SIDE


def nt(a, b):
    return lax.dot_general(a, b, (((1,), (1,)), ((), ())), preferred_element_type=F32)


def tn(a, b):
    return lax.dot_general(a, b, (((0,), (0,)), ((), ())), preferred_element_type=F32)


def nn(a, b):
    return jnp.dot(a, b, preferred_element_type=F32)


def swing(t):
    return (2 * (t % 2) - 1) * ((t + 1) // 2)


def offsets(t):
    return swing(t % SIDE), swing((t // SIDE + t) % SIDE)


def iota(axis, shape):
    return lax.broadcasted_iota(jnp.int32, shape, axis)


def ones_where(mask):
    return jnp.where(mask, 1.0, 0.0).astype(BF)


def whole(ref, sem):
    return pltpu.make_async_copy(ref, ref, sem)


def kernel(dims, tab, cnt, occ_ref, virt_ref, f_ref, out_ref, held, table, onehot, picked, got,
           got_other, pairs, spread, forth, turned, mixed, mixed_turned, back, summed, last_out,
           last_in, sem_own, xs, xr, ts, tr, fs, fr, hs, hr, bs, br, gs, gr):
    devices, aux, orbitals, slab = dims
    me = lax.axis_index("occ")
    plane = lax.axis_index("virt")
    group = plane // 2
    mirror = 3 - plane
    mate = group * 2 + 1 - plane % 2
    part_of = (plane + group) % 2
    my_y = me // (2 * SIDE)
    my_z = (me // 2) % SIDE
    my_core = me % 2
    is_host = my_core == 0
    message = 2 * aux
    tiles = message // 8
    width = aux * orbitals
    wide = 2 * slab
    part = CHUNK * aux
    block = CHUNK * tiles
    rows = SIDE * message

    barrier = pltpu.get_barrier_semaphore()

    def greet(t, c):
        pl.semaphore_signal(barrier, inc=1, device_id={"occ": (me + t) % devices})
        return c

    pl.semaphore_signal(barrier, inc=1, device_id={"virt": mirror})
    pl.semaphore_signal(barrier, inc=1, device_id={"virt": mate})
    lax.fori_loop(1, devices, greet, 0)
    pl.semaphore_wait(barrier, devices + 1)

    across = pltpu.make_async_remote_copy(f_ref, held.at[group], xs, xr, device_id={"virt": mirror})
    across.start()
    own = pltpu.make_async_copy(f_ref, held.at[group], sem_own)

    lane = iota(1, (1, 128))
    line = jnp.where(lane == 4, cnt[0], 0)
    for at, (l, s) in enumerate(((0, 0), (0, 1), (1, 0), (1, 1))):
        line = jnp.where(lane == at, tab[l, s] + 1, line)
    table[me] = line

    def tell(t, c):
        pltpu.make_async_remote_copy(
            table.at[me], table.at[me], ts, tr, device_id={"occ": (me + t) % devices}
        ).start()
        return c

    lax.fori_loop(1, devices, tell, 0)

    before = ones_where(iota(0, (128, 128)) < iota(1, (128, 128)))
    step = iota(0, (HOSTS, 1))
    fast, slow = step & 7, step >> 3
    diag = (fast + slow) & 7
    ahead_y = (((fast & 1) << 1) - 1) * ((fast + 1) >> 1)
    ahead_z = (((diag & 1) << 1) - 1) * ((diag + 1) >> 1)
    chip = ((my_y + ahead_y + SIDE) & 7) * SIDE + ((my_z + ahead_z + SIDE) & 7)
    wanted = (chip + group * HOSTS).astype(F32)
    row = iota(0, (rows, 1))
    of_host = (row * 2731) >> 16
    inside = row - of_host * message
    second = inside >= aux
    base = (jnp.where(second, inside - aux, inside) * orbitals).astype(F32) - 1.0
    spots = iota(1, (rows, width)).astype(F32)

    whole(table.at[pl.ds(0, devices - 1)], tr).wait()
    listed = table[...].reshape(devices, 128).astype(F32)
    listed_b = listed.astype(BF)
    flipped = listed.T
    count_row = flipped[4:5, :]
    rank_row = nn(jnp.broadcast_to(count_row, (16, 128)).astype(BF), before)[0:1, :]
    found0 = nn(ones_where((rank_row == wanted) & (count_row > 0.5)), listed_b)
    found1 = nn(ones_where((rank_row + 1.0 == wanted) & (count_row > 1.5)), listed_b)
    found = jnp.where(
        lane == 0,
        found0[:, 0:1] + found1[:, 2:3],
        jnp.where(lane == 1, found0[:, 1:2] + found1[:, 3:4], 0.0),
    ).astype(BF)

    own.start()
    own.wait()
    across.wait_recv()

    def select(e, c):
        spread_out = ones_where(of_host + e * SIDE == iota(1, (rows, HOSTS)))
        both = nn(spread_out, found)
        orbital = jnp.where(second, both[:, 1:2], both[:, 0:1])
        key = jnp.where(orbital > 0.5, base + orbital, -1.0)
        chosen = ones_where(spots == key)
        onehot[pl.ds(e * rows, rows)] = chosen
        picked[pl.ds(e * SIDE * tiles, SIDE * tiles)] = (
            nt(chosen, held[...].reshape(wide, width)).reshape(SIDE * tiles, 8, wide).astype(BF)
        )

        def send(u, cc):
            t = e * SIDE + u
            dy, dz = offsets(t)
            dest = (((my_y + dy + SIDE) % SIDE) * SIDE + (my_z + dz + SIDE) % SIDE) * 2
            src = picked.at[pl.ds(t * tiles, tiles)]
            dst = got.at[pl.ds((2 * t + my_core) * tiles, tiles)]

            @pl.when(dest != me)
            def _():
                pltpu.make_async_remote_copy(src, dst, fs, fr.at[e], device_id={"occ": dest}).start()

            @pl.when(dest == me)
            def _():
                pltpu.make_async_copy(src, dst, fr.at[e]).start()

            return cc

        lax.fori_loop(0, SIDE, send, 0)
        return c

    lax.fori_loop(0, SIDE, select, 0)

    def swap(e):
        spot = pl.ds(e * block, block)
        return pltpu.make_async_remote_copy(
            got.at[spot], got_other.at[spot], hs.at[e], hr.at[e], device_id={"virt": mate})

    @pl.when(is_host)
    def _():
        mine_at = (my_y * SIDE + my_z + group * HOSTS).astype(F32)
        hit0 = jnp.where((rank_row == mine_at) & (count_row > 0.5), 1.0, 0.0)
        hit1 = jnp.where((rank_row + 1.0 == mine_at) & (count_row > 1.5), 1.0, 0.0)
        first_at = jnp.sum(hit0 * flipped[0:1, :] + hit1 * flipped[2:3, :], axis=1, keepdims=True)
        second_at = jnp.sum(hit0 * flipped[1:2, :] + hit1 * flipped[3:4, :], axis=1, keepdims=True)
        names = (iota(1, (1, orbitals)) + 1).astype(F32)
        energy = jnp.sum(
            jnp.where(names == first_at, occ_ref[...], 0.0), axis=1, keepdims=True
        ) + jnp.sum(jnp.where(names == second_at, occ_ref[...], 0.0), axis=1, keepdims=True)
        virt_mine = virt_ref[pl.ds(part_of, 1), :]
        virt_other = virt_ref[pl.ds(1 - part_of, 1), :]
        virt_col = jnp.broadcast_to(virt_mine, (128, wide)).T[:, 0:1]
        spread[:, :wide] = 1.0 / (energy - virt_col - virt_mine)
        spread[:, wide:] = 1.0 / (energy - virt_col - virt_other)
        forth[...] = jnp.zeros_like(forth)
        turned[...] = jnp.zeros_like(turned)

        r = iota(0, (2 * part, 2 * part))
        low = r >= part
        q = jnp.where(low, r - part, r)
        n = (q * 5462) >> 16
        place = n * message + (q - n * aux) + jnp.where(low, 0, aux)
        sorter = ones_where(place == iota(1, (2 * part, 2 * part)))

        def collect(t, carry):
            @pl.when(t < SIDE)
            def _():
                whole(got.at[pl.ds(t * block, block)], fr.at[t]).wait()
                swap(t).start()

            @pl.when(t > 0)
            def _():
                g = t - 1
                spot = pl.ds(g * block, block)
                swap(g).wait_recv()
                mine = nn(sorter, got[spot].reshape(2 * part, wide)).astype(BF)
                other = nn(sorter, got_other[spot].reshape(2 * part, wide)).astype(BF)
                pairs[g, :, :wide] = mine
                pairs[g, :, wide:] = other
                full = jnp.concatenate([mine, other], axis=1)
                forth[...] += tn(mine[part:], full[:part])
                turned[...] += tn(mine[:part], full[part:])

            return carry

        lax.fori_loop(0, SIDE + 1, collect, 0)
        mixed[...] = ((2.0 * forth[...] - turned[...]) * spread[...]).astype(BF)
        mixed_turned[...] = ((2.0 * turned[...] - forth[...]) * spread[...]).astype(BF)

        def give(e, carry):
            both = pairs[e]
            toward_first = nt(both[:part], mixed[...]).astype(BF)
            toward_second = nt(both[part:], mixed_turned[...]).astype(BF)
            sent = jnp.concatenate([toward_second, toward_first], axis=0)
            back[pl.ds(e * block, block)] = tn(sorter, sent).reshape(block, 8, wide).astype(BF)

            def out(u, cc):
                t = e * SIDE + u // 2
                core = u % 2
                dy, dz = offsets(t)
                dest = (((my_y - dy + SIDE) % SIDE) * SIDE + (my_z - dz + SIDE) % SIDE) * 2 + core
                src = back.at[pl.ds((2 * t + core) * tiles, tiles)]
                dst = summed.at[pl.ds(t * tiles, tiles)]

                @pl.when(dest != me)
                def _():
                    pltpu.make_async_remote_copy(src, dst, bs, br, device_id={"occ": dest}).start()

                @pl.when(dest == me)
                def _():
                    pltpu.make_async_copy(src, dst, br).start()

                return cc

            lax.fori_loop(0, CHUNK, out, 0)
            return carry

        lax.fori_loop(0, SIDE, give, 0)

    whole(summed, br).wait()
    grams = tn(summed[...].reshape(HOSTS * message, wide), onehot[...])
    low_part, high_part = grams[:slab], grams[slab:]
    leaving = jnp.where(group == 0, high_part, low_part)
    last_out[...] = leaving.astype(BF)
    end = pltpu.make_async_remote_copy(last_out, last_in, gs, gr, device_id={"virt": mirror})
    end.start()
    out_ref[...] = jnp.where(group == 0, low_part, high_part)

    across.wait_send()
    whole(table.at[pl.ds(0, devices - 1)], ts).wait()

    @pl.when(is_host)
    def _():
        whole(picked.at[pl.ds(0, (HOSTS - 1) * tiles)], fs).wait()
        whole(back.at[pl.ds(0, (devices - 1) * tiles)], bs).wait()

        def sent_swap(e, c):
            swap(e).wait_send()
            return c

        lax.fori_loop(0, SIDE, sent_swap, 0)

    @pl.when(jnp.logical_not(is_host))
    def _():
        whole(picked, fs).wait()

    end.wait_recv()
    out_ref[...] += last_in[...].astype(F32)
    end.wait_send()


def body(factors, occ_energy, virt_energy, pair_table, pair_count):
    devices = lax.axis_size("occ")
    orbitals = occ_energy.shape[0]
    virtuals = virt_energy.shape[0]
    slab, width = factors.shape
    aux = width // orbitals
    message = 2 * aux
    tiles = message // 8
    wide = 2 * slab
    part = CHUNK * aux
    dims = (devices, aux, orbitals, slab)
    dma = pltpu.SemaphoreType.DMA
    vmem = pl.BlockSpec(memory_space=pltpu.VMEM)
    smem = pl.BlockSpec(memory_space=pltpu.SMEM)
    v = virt_energy.reshape(4, slab)
    virt_rows = jnp.stack([jnp.concatenate([v[0], v[3]]), jnp.concatenate([v[1], v[2]])])
    return pl.pallas_call(
        functools.partial(kernel, dims),
        out_shape=jax.ShapeDtypeStruct((slab, width), F32),
        in_specs=[smem, smem, vmem, vmem, pl.BlockSpec(memory_space=pl.ANY)],
        out_specs=vmem,
        scratch_shapes=[
            pltpu.VMEM((2, slab // 8, 8, width), BF),
            pltpu.VMEM((devices, 1, 128), jnp.int32),
            pltpu.VMEM((HOSTS * message, width), BF),
            pltpu.VMEM((HOSTS * tiles, 8, wide), BF),
            pltpu.VMEM((devices * tiles, 8, wide), BF),
            pltpu.VMEM((devices * tiles, 8, wide), BF),
            pltpu.VMEM((SIDE, 2 * part, virtuals), BF),
            pltpu.VMEM((wide, virtuals), F32),
            pltpu.VMEM((wide, virtuals), F32),
            pltpu.VMEM((wide, virtuals), F32),
            pltpu.VMEM((wide, virtuals), BF),
            pltpu.VMEM((wide, virtuals), BF),
            pltpu.VMEM((devices * tiles, 8, wide), BF),
            pltpu.VMEM((HOSTS * tiles, 8, wide), BF),
            pltpu.VMEM((slab, width), BF),
            pltpu.VMEM((slab, width), BF),
            dma(()), dma(()), dma(()), dma(()), dma(()), dma(()), dma((SIDE,)), dma((SIDE,)), dma((SIDE,)),
            dma(()), dma(()), dma(()), dma(()),
        ],
        compiler_params=pltpu.CompilerParams(
            collective_id=0, has_side_effects=True, vmem_limit_bytes=60 * 1024 * 1024
        ),
    )(pair_table, pair_count, occ_energy.reshape(1, -1), virt_rows,
      factors.reshape(slab // 8, 8, width))


def solution(mesh):
    in_specs = (P("virt", "occ"), P(), P(), P("occ", None), P("occ"))
    out_specs = P("virt", "occ")
    return jax.shard_map(body, mesh=mesh, in_specs=in_specs, out_specs=out_specs, check_vma=False)
```

```python
import functools

import jax
import jax.numpy as jnp
from jax import lax
from jax.experimental import pallas as pl
from jax.experimental.pallas import tpu as pltpu
from jax.sharding import PartitionSpec as P

BF = jnp.bfloat16
F32 = jnp.float32
SIDE = 8
HOSTS = SIDE * SIDE
CHUNK = 2 * SIDE


def nt(a, b):
    return lax.dot_general(a, b, (((1,), (1,)), ((), ())), preferred_element_type=F32)


def tn(a, b):
    return lax.dot_general(a, b, (((0,), (0,)), ((), ())), preferred_element_type=F32)


def nn(a, b):
    return jnp.dot(a, b, preferred_element_type=F32)


def swing(t):
    return (2 * (t % 2) - 1) * ((t + 1) // 2)


def offsets(t):
    return swing(t % SIDE), swing((t // SIDE + t) % SIDE)


def iota(axis, shape):
    return lax.broadcasted_iota(jnp.int32, shape, axis)


def ones_where(mask):
    return jnp.where(mask, 1.0, 0.0).astype(BF)


def whole(ref, sem):
    return pltpu.make_async_copy(ref, ref, sem)


def kernel(dims, tab, cnt, occ_ref, virt_ref, f_ref, out_ref, add_ref, held, table, onehot1, onehot2, picked, got,
           got_other, pairs, spread, forth, turned, mixed, mixed_turned, back, summed1, summed2, out1, out2,
           in1, in2, sem_own, xs, xr, ts, tr, fs, fr, hs, hr, bs, br, gs, gr, ps, pr, ls, lr):
    devices, aux, orbitals, slab = dims
    me = lax.axis_index("occ")
    plane = lax.axis_index("virt")
    group = plane // 2
    mirror = 3 - plane
    mate = group * 2 + 1 - plane % 2
    part_of = (plane + group) % 2
    my_y = me // (2 * SIDE)
    my_z = (me // 2) % SIDE
    my_core = me % 2
    is_host = my_core == 0
    lead = me - my_core
    twin = me + 1 - 2 * my_core
    message = 2 * aux
    tiles = message // 8
    width = aux * orbitals
    wide = 2 * slab
    part = CHUNK * aux
    block = CHUNK * tiles
    rows = SIDE * message

    barrier = pltpu.get_barrier_semaphore()

    def greet(t, c):
        pl.semaphore_signal(barrier, inc=1, device_id={"occ": (me + t) % devices})
        return c

    pl.semaphore_signal(barrier, inc=1, device_id={"virt": mirror})
    pl.semaphore_signal(barrier, inc=1, device_id={"virt": mate})
    pl.semaphore_signal(barrier, inc=1, device_id={"occ": twin, "virt": mate})
    lax.fori_loop(1, devices, greet, 0)
    pl.semaphore_wait(barrier, devices + 2)

    across = pltpu.make_async_remote_copy(f_ref, held.at[group], xs, xr, device_id={"virt": mirror})
    across.start()
    own = pltpu.make_async_copy(f_ref, held.at[group], sem_own)

    lane = iota(1, (1, 128))
    line = jnp.where(lane == 4, cnt[0], 0)
    for at, (l, s) in enumerate(((0, 0), (0, 1), (1, 0), (1, 1))):
        line = jnp.where(lane == at, tab[l, s] + 1, line)
    table[me] = line

    def tell(t, c):
        pltpu.make_async_remote_copy(
            table.at[me], table.at[me], ts, tr, device_id={"occ": (me + t) % devices}
        ).start()
        return c

    lax.fori_loop(1, devices, tell, 0)

    before = ones_where(iota(0, (128, 128)) < iota(1, (128, 128)))
    step = iota(0, (HOSTS, 1))
    fast, slow = step & 7, step >> 3
    diag = (fast + slow) & 7
    ahead_y = (((fast & 1) << 1) - 1) * ((fast + 1) >> 1)
    ahead_z = (((diag & 1) << 1) - 1) * ((diag + 1) >> 1)
    chip = ((my_y + ahead_y + SIDE) & 7) * SIDE + ((my_z + ahead_z + SIDE) & 7)
    wanted = (chip + group * HOSTS).astype(F32)
    row = iota(0, (rows, 1))
    of_host = (row * 2731) >> 16
    inside = row - of_host * message
    second = (inside & 1) > 0
    base = ((inside >> 1) * orbitals).astype(F32) - 1.0
    spots = iota(1, (rows, width)).astype(F32)
    edge = SIDE * 16
    late = row >= edge
    host2 = jnp.where(late, (row - edge) >> 3, row >> 4)
    inside2 = jnp.where(late, 16 + (row & 7), row & 15)
    second2 = (inside2 & 1) > 0
    base2 = ((inside2 >> 1) * orbitals).astype(F32) - 1.0
    head = 8 * orbitals
    rest = width - head

    whole(table.at[pl.ds(0, devices - 1)], tr).wait()
    listed = table[...].reshape(devices, 128).astype(F32)
    listed_b = listed.astype(BF)
    flipped = listed.T
    count_row = flipped[4:5, :]
    rank_row = nn(jnp.broadcast_to(count_row, (16, 128)).astype(BF), before)[0:1, :]
    found0 = nn(ones_where((rank_row == wanted) & (count_row > 0.5)), listed_b)
    found1 = nn(ones_where((rank_row + 1.0 == wanted) & (count_row > 1.5)), listed_b)
    found = jnp.where(
        lane == 0,
        found0[:, 0:1] + found1[:, 2:3],
        jnp.where(lane == 1, found0[:, 1:2] + found1[:, 3:4], 0.0),
    ).astype(BF)

    own.start()
    own.wait()
    across.wait_recv()

    def slot(t, core):
        return pl.ds(((t // SIDE) * CHUNK + core * SIDE + t % SIDE) * tiles, tiles)

    def select(e, c):
        def keys(host, odd, start):
            both = nn(ones_where(host + e * SIDE == iota(1, (rows, HOSTS))), found)
            orbital = jnp.where(odd, both[:, 1:2], both[:, 0:1])
            return jnp.where(orbital > 0.5, start + orbital, -1.0)

        chosen = ones_where(spots == keys(of_host, second, base))
        picked[pl.ds(e * SIDE * tiles, SIDE * tiles)] = (
            nt(chosen, held[...].reshape(wide, width)).reshape(SIDE * tiles, 8, wide).astype(BF)
        )

        def send(u, cc):
            t = e * SIDE + u
            dy, dz = offsets(t)
            dest = (((my_y + dy + SIDE) % SIDE) * SIDE + (my_z + dz + SIDE) % SIDE) * 2 + my_core
            src = picked.at[pl.ds(t * tiles, tiles)]
            dst = got.at[slot(t, my_core)]

            @pl.when(dest != me)
            def _():
                pltpu.make_async_remote_copy(src, dst, fs, fr.at[t], device_id={"occ": dest}).start()

            @pl.when(dest == me)
            def _():
                pltpu.make_async_copy(src, dst, fr.at[t]).start()

            return cc

        lax.fori_loop(0, SIDE, send, 0)
        key2 = keys(host2, second2, base2)
        onehot1[pl.ds(e * edge, edge)] = ones_where(spots[:edge, :head] == key2[:edge])
        onehot2[pl.ds(e * (rows - edge), rows - edge)] = ones_where(spots[:rows - edge, head:] == key2[edge:])
        return c

    lax.fori_loop(0, SIDE, select, 0)

    def pass_on(t):
        spot = slot(t, my_core)
        whole(got.at[spot], fr.at[t]).wait()
        pltpu.make_async_remote_copy(
            got.at[spot], got_other.at[spot], hs, hr.at[t // SIDE], device_id={"occ": lead, "virt": mate}
        ).start()

    def beside(e):
        spot = pl.ds((e * CHUNK + SIDE) * tiles, SIDE * tiles)
        return pltpu.make_async_remote_copy(
            back.at[spot], back.at[spot], ps, pr.at[e], device_id={"occ": twin})

    def give_out(e, phase):
        def out(u, cc):
            t = e * SIDE + u
            dy, dz = offsets(t)
            dest = (((my_y - dy + SIDE) % SIDE) * SIDE + (my_z - dz + SIDE) % SIDE) * 2 + my_core
            first_tile = ((t // SIDE) * CHUNK + my_core * SIDE + t % SIDE) * tiles
            if phase == 0:
                src, dst = back.at[pl.ds(first_tile, 2)], summed1.at[pl.ds(t * 2, 2)]
            else:
                src, dst = back.at[pl.ds(first_tile + 2, 1)], summed2.at[pl.ds(t, 1)]

            @pl.when(dest != me)
            def _():
                pltpu.make_async_remote_copy(src, dst, bs, br.at[phase], device_id={"occ": dest}).start()

            @pl.when(dest == me)
            def _():
                pltpu.make_async_copy(src, dst, br.at[phase]).start()

            return cc

        lax.fori_loop(0, SIDE, out, 0)

    def give_late(e, c):
        give_out(e, 1)
        return c

    @pl.when(jnp.logical_not(is_host))
    def _():
        def relay(t, c):
            pass_on(t)
            spot = slot(t, 1)
            pltpu.make_async_remote_copy(
                got.at[spot], got.at[spot], ls, lr.at[t // SIDE], device_id={"occ": lead}).start()
            return c

        lax.fori_loop(0, HOSTS, relay, 0)

        def relay_out(e, c):
            beside(e).wait_recv()
            give_out(e, 0)
            return c

        lax.fori_loop(0, SIDE, relay_out, 0)

    @pl.when(is_host)
    def _():
        mine_at = (my_y * SIDE + my_z + group * HOSTS).astype(F32)
        hit0 = jnp.where((rank_row == mine_at) & (count_row > 0.5), 1.0, 0.0)
        hit1 = jnp.where((rank_row + 1.0 == mine_at) & (count_row > 1.5), 1.0, 0.0)
        first_at = jnp.sum(hit0 * flipped[0:1, :] + hit1 * flipped[2:3, :], axis=1, keepdims=True)
        second_at = jnp.sum(hit0 * flipped[1:2, :] + hit1 * flipped[3:4, :], axis=1, keepdims=True)
        names = (iota(1, (1, orbitals)) + 1).astype(F32)
        energy = jnp.sum(
            jnp.where(names == first_at, occ_ref[...], 0.0), axis=1, keepdims=True
        ) + jnp.sum(jnp.where(names == second_at, occ_ref[...], 0.0), axis=1, keepdims=True)
        virt_mine = virt_ref[pl.ds(part_of, 1), :]
        virt_other = virt_ref[pl.ds(1 - part_of, 1), :]
        virt_col = jnp.broadcast_to(virt_mine, (128, wide)).T[:, 0:1]
        spread[:, :wide] = 1.0 / (energy - virt_col - virt_mine)
        spread[:, wide:] = 1.0 / (energy - virt_col - virt_other)
        forth[...] = jnp.zeros_like(forth)
        turned[...] = jnp.zeros_like(turned)

        r = iota(0, (2 * part, 2 * part))
        low = r >= part
        q = jnp.where(low, r - part, r)
        n = (q * 5462) >> 16
        place = n * message + 2 * (q - n * aux) + jnp.where(low, 0, 1)
        sorter = ones_where(place == iota(1, (2 * part, 2 * part)))

        def collect(t, carry):
            @pl.when(t < SIDE)
            def _():
                def forward(u, cc):
                    pass_on(t * SIDE + u)
                    return cc

                lax.fori_loop(0, SIDE, forward, 0)

            @pl.when(t > 0)
            def _():
                g = t - 1
                spot = pl.ds(g * block, block)
                whole(got.at[pl.ds(0, SIDE * tiles)], lr.at[g]).wait()
                whole(got_other.at[spot], hr.at[g]).wait()
                mine = nn(sorter, got[spot].reshape(2 * part, wide)).astype(BF)
                other = nn(sorter, got_other[spot].reshape(2 * part, wide)).astype(BF)
                pairs[g, :, :wide] = mine
                pairs[g, :, wide:] = other
                full = jnp.concatenate([mine, other], axis=1)
                forth[...] += tn(mine[part:], full[:part])
                turned[...] += tn(mine[:part], full[part:])

            return carry

        lax.fori_loop(0, SIDE + 1, collect, 0)
        mixed[...] = ((2.0 * forth[...] - turned[...]) * spread[...]).astype(BF)
        mixed_turned[...] = ((2.0 * turned[...] - forth[...]) * spread[...]).astype(BF)

        def give(e, carry):
            both = pairs[e]
            toward_first = nt(both[:part], mixed[...]).astype(BF)
            toward_second = nt(both[part:], mixed_turned[...]).astype(BF)
            sent = jnp.concatenate([toward_second, toward_first], axis=0)
            back[pl.ds(e * block, block)] = tn(sorter, sent).reshape(block, 8, wide).astype(BF)

            beside(e).start()
            give_out(e, 0)
            return carry

        lax.fori_loop(0, SIDE, give, 0)

    lax.fori_loop(0, SIDE, give_late, 0)

    def finish(phase, summed, onehot, leaving, arriving, columns):
        whole(summed, br.at[phase]).wait()
        grams = tn(summed[...].reshape(onehot.shape[0], wide), onehot[...])
        low_part, high_part = grams[:slab], grams[slab:]
        leaving[...] = jnp.where(group == 0, high_part, low_part).astype(BF)
        pltpu.make_async_remote_copy(
            leaving, arriving, gs.at[phase], gr.at[phase], device_id={"virt": mirror}).start()
        out_ref[:, columns] = jnp.where(group == 0, low_part, high_part)

    finish(0, summed1, onehot1, out1, in1, pl.ds(0, head))
    finish(1, summed2, onehot2, out2, in2, pl.ds(head, rest))

    across.wait_send()
    whole(table.at[pl.ds(0, devices - 1)], ts).wait()

    whole(picked.at[pl.ds(0, (HOSTS - 1) * tiles)], fs).wait()
    whole(back.at[pl.ds(0, (HOSTS - 1) * tiles)], bs).wait()
    whole(got.at[pl.ds(0, HOSTS * tiles)], hs).wait()

    @pl.when(is_host)
    def _():
        whole(back.at[pl.ds(0, HOSTS * tiles)], ps).wait()

    @pl.when(jnp.logical_not(is_host))
    def _():
        whole(got.at[pl.ds(0, HOSTS * tiles)], ls).wait()

    whole(in1, gr.at[0]).wait()
    add_ref[:, :head] = in1[...]
    whole(in2, gr.at[1]).wait()
    add_ref[:, head:] = in2[...]
    whole(out1, gs.at[0]).wait()
    whole(out2, gs.at[1]).wait()


def body(factors, occ_energy, virt_energy, pair_table, pair_count):
    devices = lax.axis_size("occ")
    orbitals = occ_energy.shape[0]
    virtuals = virt_energy.shape[0]
    slab, width = factors.shape
    aux = width // orbitals
    message = 2 * aux
    tiles = message // 8
    wide = 2 * slab
    part = CHUNK * aux
    dims = (devices, aux, orbitals, slab)
    dma = pltpu.SemaphoreType.DMA
    vmem = pl.BlockSpec(memory_space=pltpu.VMEM)
    smem = pl.BlockSpec(memory_space=pltpu.SMEM)
    v = virt_energy.reshape(4, slab)
    virt_rows = jnp.stack([jnp.concatenate([v[0], v[3]]), jnp.concatenate([v[1], v[2]])])
    head = 8 * orbitals
    own, other = pl.pallas_call(
        functools.partial(kernel, dims),
        out_shape=(jax.ShapeDtypeStruct((slab, width), F32), jax.ShapeDtypeStruct((slab, width), BF)),
        in_specs=[smem, smem, vmem, vmem, pl.BlockSpec(memory_space=pl.ANY)],
        out_specs=(vmem, vmem),
        scratch_shapes=[
            pltpu.VMEM((2, slab // 8, 8, width), BF),
            pltpu.VMEM((devices, 1, 128), jnp.int32),
            pltpu.VMEM((HOSTS * 16, head), BF),
            pltpu.VMEM((HOSTS * 8, width - head), BF),
            pltpu.VMEM((HOSTS * tiles, 8, wide), BF),
            pltpu.VMEM((devices * tiles, 8, wide), BF),
            pltpu.VMEM((devices * tiles, 8, wide), BF),
            pltpu.VMEM((SIDE, 2 * part, virtuals), BF),
            pltpu.VMEM((wide, virtuals), F32),
            pltpu.VMEM((wide, virtuals), F32),
            pltpu.VMEM((wide, virtuals), F32),
            pltpu.VMEM((wide, virtuals), BF),
            pltpu.VMEM((wide, virtuals), BF),
            pltpu.VMEM((devices * tiles, 8, wide), BF),
            pltpu.VMEM((HOSTS * 2, 8, wide), BF),
            pltpu.VMEM((HOSTS, 8, wide), BF),
            pltpu.VMEM((slab, head), BF),
            pltpu.VMEM((slab, width - head), BF),
            pltpu.VMEM((slab, head), BF),
            pltpu.VMEM((slab, width - head), BF),
            dma(()), dma(()), dma(()), dma(()), dma(()), dma(()), dma((HOSTS,)), dma(()), dma((SIDE,)),
            dma(()), dma((2,)), dma((2,)), dma((2,)), dma(()), dma((SIDE,)), dma(()), dma((SIDE,)),
        ],
        compiler_params=pltpu.CompilerParams(
            collective_id=0, has_side_effects=True, vmem_limit_bytes=60 * 1024 * 1024
        ),
    )(pair_table, pair_count, occ_energy.reshape(1, -1), virt_rows,
      factors.reshape(slab // 8, 8, width))
    return own + other.astype(F32)


def solution(mesh):
    in_specs = (P("virt", "occ"), P(), P(), P("occ", None), P("occ"))
    out_specs = P("virt", "occ")
    return jax.shard_map(body, mesh=mesh, in_specs=in_specs, out_specs=out_specs, check_vma=False)
```

```python
import functools

import jax
import jax.numpy as jnp
from jax import lax
from jax.experimental import pallas as pl
from jax.experimental.pallas import tpu as pltpu
from jax.sharding import PartitionSpec as P

BF = jnp.bfloat16
F32 = jnp.float32
SIDE = 8
HOSTS = SIDE * SIDE
CHUNK = 2 * SIDE


def nt(a, b):
    return lax.dot_general(a, b, (((1,), (1,)), ((), ())), preferred_element_type=F32)


def tn(a, b):
    return lax.dot_general(a, b, (((0,), (0,)), ((), ())), preferred_element_type=F32)


def nn(a, b):
    return jnp.dot(a, b, preferred_element_type=F32)


def swing(t):
    return (2 * (t % 2) - 1) * ((t + 1) // 2)


def offsets(t):
    return swing(t % SIDE), swing((t // SIDE + 5 * t) % SIDE)


def iota(axis, shape):
    return lax.broadcasted_iota(jnp.int32, shape, axis)


def ones_where(mask):
    return jnp.where(mask, 1.0, 0.0).astype(BF)


def whole(ref, sem):
    return pltpu.make_async_copy(ref, ref, sem)


def kernel(dims, tab, cnt, occ_ref, virt_ref, f_ref, out_ref, add_ref, held, table, onehot1, onehot2, picked, got,
           got_other, pairs, spread, forth, turned, mixed, mixed_turned, back, summed1, summed2, out1, out2,
           in1, in2, sem_own, xs, xr, ts, tr, fs, fr, hs, hr, bs, br, gs, gr, ps, pr, ls, lr):
    devices, aux, orbitals, slab = dims
    me = lax.axis_index("occ")
    plane = lax.axis_index("virt")
    group = plane // 2
    mirror = 3 - plane
    mate = group * 2 + 1 - plane % 2
    part_of = (plane + group) % 2
    my_y = me // (2 * SIDE)
    my_z = (me // 2) % SIDE
    my_core = me % 2
    is_host = my_core == 0
    way = 1 - 2 * my_core
    lead = me - my_core
    twin = me + 1 - 2 * my_core
    message = 2 * aux
    tiles = message // 8
    width = aux * orbitals
    wide = 2 * slab
    part = CHUNK * aux
    block = CHUNK * tiles
    rows = SIDE * message

    barrier = pltpu.get_barrier_semaphore()

    def greet(t, c):
        pl.semaphore_signal(barrier, inc=1, device_id={"occ": (me + t) % devices})
        return c

    pl.semaphore_signal(barrier, inc=1, device_id={"virt": mirror})
    pl.semaphore_signal(barrier, inc=1, device_id={"virt": mate})
    pl.semaphore_signal(barrier, inc=1, device_id={"occ": twin, "virt": mate})
    lax.fori_loop(1, devices, greet, 0)
    pl.semaphore_wait(barrier, devices + 2)

    across = pltpu.make_async_remote_copy(f_ref, held.at[group], xs, xr, device_id={"virt": mirror})
    across.start()
    own = pltpu.make_async_copy(f_ref, held.at[group], sem_own)

    lane = iota(1, (1, 128))
    line = jnp.where(lane == 4, cnt[0], 0)
    for at, (l, s) in enumerate(((0, 0), (0, 1), (1, 0), (1, 1))):
        line = jnp.where(lane == at, tab[l, s] + 1, line)
    table[me] = line

    def tell(t, c):
        pltpu.make_async_remote_copy(
            table.at[me], table.at[me], ts, tr, device_id={"occ": (me + t) % devices}
        ).start()
        return c

    lax.fori_loop(1, devices, tell, 0)

    before = ones_where(iota(0, (128, 128)) < iota(1, (128, 128)))
    step = iota(0, (HOSTS, 1))
    fast, slow = step & 7, step >> 3
    diag = (5 * fast + slow) & 7
    ahead_y = (((fast & 1) << 1) - 1) * ((fast + 1) >> 1)
    ahead_z = (((diag & 1) << 1) - 1) * ((diag + 1) >> 1)
    chip = ((my_y + way * ahead_y + SIDE) & 7) * SIDE + ((my_z + way * ahead_z + SIDE) & 7)
    wanted = (chip + group * HOSTS).astype(F32)
    row = iota(0, (rows, 1))
    of_host = (row * 2731) >> 16
    inside = row - of_host * message
    second = (inside & 1) > 0
    base = ((inside >> 1) * orbitals).astype(F32) - 1.0
    spots = iota(1, (rows, width)).astype(F32)
    edge = SIDE * 16
    late = row >= edge
    host2 = jnp.where(late, (row - edge) >> 3, row >> 4)
    inside2 = jnp.where(late, 16 + (row & 7), row & 15)
    second2 = (inside2 & 1) > 0
    base2 = ((inside2 >> 1) * orbitals).astype(F32) - 1.0
    head = 8 * orbitals
    rest = width - head

    whole(table.at[pl.ds(0, devices - 1)], tr).wait()
    listed = table[...].reshape(devices, 128).astype(F32)
    listed_b = listed.astype(BF)
    flipped = listed.T
    count_row = flipped[4:5, :]
    rank_row = nn(jnp.broadcast_to(count_row, (16, 128)).astype(BF), before)[0:1, :]
    found0 = nn(ones_where((rank_row == wanted) & (count_row > 0.5)), listed_b)
    found1 = nn(ones_where((rank_row + 1.0 == wanted) & (count_row > 1.5)), listed_b)
    found = jnp.where(
        lane == 0,
        found0[:, 0:1] + found1[:, 2:3],
        jnp.where(lane == 1, found0[:, 1:2] + found1[:, 3:4], 0.0),
    ).astype(BF)

    own.start()
    own.wait()
    across.wait_recv()

    def slot(t, core):
        return pl.ds(((t // SIDE) * CHUNK + core * SIDE + t % SIDE) * tiles, tiles)

    def select(e, c):
        def keys(host, odd, start):
            both = nn(ones_where(host + e * SIDE == iota(1, (rows, HOSTS))), found)
            orbital = jnp.where(odd, both[:, 1:2], both[:, 0:1])
            return jnp.where(orbital > 0.5, start + orbital, -1.0)

        chosen = ones_where(spots == keys(of_host, second, base))
        picked[pl.ds(e * SIDE * tiles, SIDE * tiles)] = (
            nt(chosen, held[...].reshape(wide, width)).reshape(SIDE * tiles, 8, wide).astype(BF)
        )

        def send(u, cc):
            t = e * SIDE + u
            dy, dz = offsets(t)
            dest = (((my_y + way * dy + SIDE) % SIDE) * SIDE + (my_z + way * dz + SIDE) % SIDE) * 2 + my_core
            src = picked.at[pl.ds(t * tiles, tiles)]
            dst = got.at[slot(t, my_core)]

            @pl.when(dest != me)
            def _():
                pltpu.make_async_remote_copy(src, dst, fs, fr.at[t], device_id={"occ": dest}).start()

            @pl.when(dest == me)
            def _():
                pltpu.make_async_copy(src, dst, fr.at[t]).start()

            return cc

        lax.fori_loop(0, SIDE, send, 0)
        key2 = keys(host2, second2, base2)
        onehot1[pl.ds(e * edge, edge)] = ones_where(spots[:edge, :head] == key2[:edge])
        onehot2[pl.ds(e * (rows - edge), rows - edge)] = ones_where(spots[:rows - edge, head:] == key2[edge:])
        return c

    lax.fori_loop(0, SIDE, select, 0)

    def pass_on(t):
        spot = slot(t, my_core)
        whole(got.at[spot], fr.at[t]).wait()
        pltpu.make_async_remote_copy(
            got.at[spot], got_other.at[spot], hs, hr.at[t // SIDE], device_id={"occ": lead, "virt": mate}
        ).start()

    def beside(e):
        spot = pl.ds((e * CHUNK + SIDE) * tiles, SIDE * tiles)
        return pltpu.make_async_remote_copy(
            back.at[spot], back.at[spot], ps, pr.at[e], device_id={"occ": twin})

    def give_out(e, phase):
        def out(u, cc):
            t = e * SIDE + u
            dy, dz = offsets(t)
            dest = (((my_y - way * dy + SIDE) % SIDE) * SIDE + (my_z - way * dz + SIDE) % SIDE) * 2 + my_core
            first_tile = ((t // SIDE) * CHUNK + my_core * SIDE + t % SIDE) * tiles
            if phase == 0:
                src, dst = back.at[pl.ds(first_tile, 2)], summed1.at[pl.ds(t * 2, 2)]
            else:
                src, dst = back.at[pl.ds(first_tile + 2, 1)], summed2.at[pl.ds(t, 1)]

            @pl.when(dest != me)
            def _():
                pltpu.make_async_remote_copy(src, dst, bs, br.at[phase], device_id={"occ": dest}).start()

            @pl.when(dest == me)
            def _():
                pltpu.make_async_copy(src, dst, br.at[phase]).start()

            return cc

        lax.fori_loop(0, SIDE, out, 0)

    def give_late(e, c):
        give_out(e, 1)
        return c

    @pl.when(jnp.logical_not(is_host))
    def _():
        def relay(t, c):
            pass_on(t)
            spot = slot(t, 1)
            pltpu.make_async_remote_copy(
                got.at[spot], got.at[spot], ls, lr.at[t // SIDE], device_id={"occ": lead}).start()
            return c

        lax.fori_loop(0, HOSTS, relay, 0)

        def relay_out(e, c):
            beside(e).wait_recv()
            give_out(e, 0)
            return c

        lax.fori_loop(0, SIDE, relay_out, 0)

    @pl.when(is_host)
    def _():
        mine_at = (my_y * SIDE + my_z + group * HOSTS).astype(F32)
        hit0 = jnp.where((rank_row == mine_at) & (count_row > 0.5), 1.0, 0.0)
        hit1 = jnp.where((rank_row + 1.0 == mine_at) & (count_row > 1.5), 1.0, 0.0)
        first_at = jnp.sum(hit0 * flipped[0:1, :] + hit1 * flipped[2:3, :], axis=1, keepdims=True)
        second_at = jnp.sum(hit0 * flipped[1:2, :] + hit1 * flipped[3:4, :], axis=1, keepdims=True)
        names = (iota(1, (1, orbitals)) + 1).astype(F32)
        energy = jnp.sum(
            jnp.where(names == first_at, occ_ref[...], 0.0), axis=1, keepdims=True
        ) + jnp.sum(jnp.where(names == second_at, occ_ref[...], 0.0), axis=1, keepdims=True)
        virt_mine = virt_ref[pl.ds(part_of, 1), :]
        virt_other = virt_ref[pl.ds(1 - part_of, 1), :]
        virt_col = jnp.broadcast_to(virt_mine, (128, wide)).T[:, 0:1]
        spread[:, :wide] = 1.0 / (energy - virt_col - virt_mine)
        spread[:, wide:] = 1.0 / (energy - virt_col - virt_other)
        forth[...] = jnp.zeros_like(forth)
        turned[...] = jnp.zeros_like(turned)

        r = iota(0, (2 * part, 2 * part))
        low = r >= part
        q = jnp.where(low, r - part, r)
        n = (q * 5462) >> 16
        place = n * message + 2 * (q - n * aux) + jnp.where(low, 0, 1)
        sorter = ones_where(place == iota(1, (2 * part, 2 * part)))

        def collect(t, carry):
            @pl.when(t < SIDE)
            def _():
                def forward(u, cc):
                    pass_on(t * SIDE + u)
                    return cc

                lax.fori_loop(0, SIDE, forward, 0)

            @pl.when(t > 0)
            def _():
                g = t - 1
                spot = pl.ds(g * block, block)
                whole(got.at[pl.ds(0, SIDE * tiles)], lr.at[g]).wait()
                whole(got_other.at[spot], hr.at[g]).wait()
                mine = nn(sorter, got[spot].reshape(2 * part, wide)).astype(BF)
                other = nn(sorter, got_other[spot].reshape(2 * part, wide)).astype(BF)
                pairs[g, :, :wide] = mine
                pairs[g, :, wide:] = other
                full = jnp.concatenate([mine, other], axis=1)
                forth[...] += tn(mine[part:], full[:part])
                turned[...] += tn(mine[:part], full[part:])

            return carry

        lax.fori_loop(0, SIDE + 1, collect, 0)
        mixed[...] = ((2.0 * forth[...] - turned[...]) * spread[...]).astype(BF)
        mixed_turned[...] = ((2.0 * turned[...] - forth[...]) * spread[...]).astype(BF)

        def give(e, carry):
            both = pairs[e]
            toward_first = nt(both[:part], mixed[...]).astype(BF)
            toward_second = nt(both[part:], mixed_turned[...]).astype(BF)
            sent = jnp.concatenate([toward_second, toward_first], axis=0)
            back[pl.ds(e * block, block)] = tn(sorter, sent).reshape(block, 8, wide).astype(BF)

            beside(e).start()
            give_out(e, 0)
            return carry

        lax.fori_loop(0, SIDE, give, 0)

    lax.fori_loop(0, SIDE, give_late, 0)

    def finish(phase, summed, onehot, leaving, arriving, columns):
        whole(summed, br.at[phase]).wait()
        grams = tn(summed[...].reshape(onehot.shape[0], wide), onehot[...])
        low_part, high_part = grams[:slab], grams[slab:]
        leaving[...] = jnp.where(group == 0, high_part, low_part).astype(BF)
        pltpu.make_async_remote_copy(
            leaving, arriving, gs.at[phase], gr.at[phase], device_id={"virt": mirror}).start()
        out_ref[:, columns] = jnp.where(group == 0, low_part, high_part)

    finish(0, summed1, onehot1, out1, in1, pl.ds(0, head))
    finish(1, summed2, onehot2, out2, in2, pl.ds(head, rest))

    across.wait_send()
    whole(table.at[pl.ds(0, devices - 1)], ts).wait()

    whole(picked.at[pl.ds(0, (HOSTS - 1) * tiles)], fs).wait()
    whole(back.at[pl.ds(0, (HOSTS - 1) * tiles)], bs).wait()
    whole(got.at[pl.ds(0, HOSTS * tiles)], hs).wait()

    @pl.when(is_host)
    def _():
        whole(back.at[pl.ds(0, HOSTS * tiles)], ps).wait()

    @pl.when(jnp.logical_not(is_host))
    def _():
        whole(got.at[pl.ds(0, HOSTS * tiles)], ls).wait()

    whole(in1, gr.at[0]).wait()
    add_ref[:, :head] = in1[...]
    whole(in2, gr.at[1]).wait()
    add_ref[:, head:] = in2[...]
    whole(out1, gs.at[0]).wait()
    whole(out2, gs.at[1]).wait()


def body(factors, occ_energy, virt_energy, pair_table, pair_count):
    devices = lax.axis_size("occ")
    orbitals = occ_energy.shape[0]
    virtuals = virt_energy.shape[0]
    slab, width = factors.shape
    aux = width // orbitals
    message = 2 * aux
    tiles = message // 8
    wide = 2 * slab
    part = CHUNK * aux
    dims = (devices, aux, orbitals, slab)
    dma = pltpu.SemaphoreType.DMA
    vmem = pl.BlockSpec(memory_space=pltpu.VMEM)
    smem = pl.BlockSpec(memory_space=pltpu.SMEM)
    v = virt_energy.reshape(4, slab)
    virt_rows = jnp.stack([jnp.concatenate([v[0], v[3]]), jnp.concatenate([v[1], v[2]])])
    head = 8 * orbitals
    own, other = pl.pallas_call(
        functools.partial(kernel, dims),
        out_shape=(jax.ShapeDtypeStruct((slab, width), F32), jax.ShapeDtypeStruct((slab, width), BF)),
        in_specs=[smem, smem, vmem, vmem, pl.BlockSpec(memory_space=pl.ANY)],
        out_specs=(vmem, vmem),
        scratch_shapes=[
            pltpu.VMEM((2, slab // 8, 8, width), BF),
            pltpu.VMEM((devices, 1, 128), jnp.int32),
            pltpu.VMEM((HOSTS * 16, head), BF),
            pltpu.VMEM((HOSTS * 8, width - head), BF),
            pltpu.VMEM((HOSTS * tiles, 8, wide), BF),
            pltpu.VMEM((devices * tiles, 8, wide), BF),
            pltpu.VMEM((devices * tiles, 8, wide), BF),
            pltpu.VMEM((SIDE, 2 * part, virtuals), BF),
            pltpu.VMEM((wide, virtuals), F32),
            pltpu.VMEM((wide, virtuals), F32),
            pltpu.VMEM((wide, virtuals), F32),
            pltpu.VMEM((wide, virtuals), BF),
            pltpu.VMEM((wide, virtuals), BF),
            pltpu.VMEM((devices * tiles, 8, wide), BF),
            pltpu.VMEM((HOSTS * 2, 8, wide), BF),
            pltpu.VMEM((HOSTS, 8, wide), BF),
            pltpu.VMEM((slab, head), BF),
            pltpu.VMEM((slab, width - head), BF),
            pltpu.VMEM((slab, head), BF),
            pltpu.VMEM((slab, width - head), BF),
            dma(()), dma(()), dma(()), dma(()), dma(()), dma(()), dma((HOSTS,)), dma(()), dma((SIDE,)),
            dma(()), dma((2,)), dma((2,)), dma((2,)), dma(()), dma((SIDE,)), dma(()), dma((SIDE,)),
        ],
        compiler_params=pltpu.CompilerParams(
            collective_id=0, has_side_effects=True, vmem_limit_bytes=60 * 1024 * 1024
        ),
    )(pair_table, pair_count, occ_energy.reshape(1, -1), virt_rows,
      factors.reshape(slab // 8, 8, width))
    return own + other.astype(F32)


def solution(mesh):
    in_specs = (P("virt", "occ"), P(), P(), P("occ", None), P("occ"))
    out_specs = P("virt", "occ")
    return jax.shard_map(body, mesh=mesh, in_specs=in_specs, out_specs=out_specs, check_vma=False)
```
